32 devices in a mesh: seq: 8 (over y, x, core), tensor: 4 (over z).
Axes of the slice: x: 2, y: 2, z: 4, core: 2. Of those that a mesh axis runs over, the one named last changes fastest.
Arguments:
- tokens: bfloat16 [4096, 2048], P('seq'), may hold values from -200 to 200
- w_latent: bfloat16 [2048, 512], P(None, 'tensor'), may hold values from -0.125 to 0.125
- w_query: bfloat16 [2048, 2048], P(None, 'tensor'), may hold values from -0.125 to 0.125
- w_key_up: bfloat16 [512, 2048], P(None, 'tensor'), may hold values from -0.25 to 0.25
- w_value_up: bfloat16 [512, 2048], P(None, 'tensor'), may hold values from -0.25 to 0.25
- w_stu_query: bfloat16 [2048, 2048], P(None, 'tensor'), may hold values from -0.125 to 0.125
- w_stu_key: bfloat16 [2048, 2048], P(None, 'tensor'), may hold values from -0.125 to 0.125
- w_stu_value: bfloat16 [2048, 2048], P(None, 'tensor'), may hold values from -0.125 to 0.125
- forget: float32 [4096, 16], P('seq', 'tensor'), may hold values from -1 to 0
Outputs:
- teacher_out: bfloat16 [4096, 2048], P('seq', 'tensor')
- loss_mean: float32 [], replicated
- weight_grad: float32 [2048, 2048], P('seq', 'tensor')
The draws below stay inside these ranges and needn't reach their ends.
All inputs are finite; a program needn't handle non-finite values.
Results may differ from the reference program's by a relative error of at most 0.02.
The reference program's roundings to bfloat16 on the way (of `latent`, `queries`, `weights` and `value_grad`) count: a program that leaves them out, or rounds other values in their place, can miss the bound.
Values may be sent and summed in bfloat16 or wider, within the bound.
No kernel may reach another device: no remote copies, remote signals or barrier semaphores. Data moves between devices by JAX's collectives and lax.ppermute only.
A program may use at most 64 MiB of HBM per device.

```python
import math
import jax
import jax.numpy as jnp
from jax import lax

D = 2048
HEAD_COUNT = 16
DH = 128
LAT = 512
TOK_DEV = 512
TOKEN_COUNT = 4096


def draw_tokens(key, part):
    base = jax.random.truncated_normal(jax.random.fold_in(key, 11), -6.0, 6.0, (TOKEN_COUNT, D), jnp.float32)
    return base.astype(jnp.bfloat16)


def draw_forget(key, part):
    keep_share = 0.5
    slow_heads = jax.random.uniform(jax.random.fold_in(key, 21), (1, HEAD_COUNT), jnp.float32) < keep_share
    slow_rate = jnp.exp(jax.random.uniform(jax.random.fold_in(key, 22), (1, HEAD_COUNT), jnp.float32, math.log(0.03), math.log(0.15))) / TOKEN_COUNT
    fast_rate = jnp.exp(jax.random.uniform(jax.random.fold_in(key, 23), (1, HEAD_COUNT), jnp.float32, math.log(1.0 / 50.0), math.log(1.0 / 30.0)))
    head_decay_rate = jnp.where(slow_heads, slow_rate, fast_rate)
    random_perturbation = jnp.exp(jax.random.uniform(jax.random.fold_in(key, 24), (TOKEN_COUNT, HEAD_COUNT), jnp.float32, math.log(0.5), math.log(2.0)))
    block_scale = jnp.exp(jax.random.uniform(jax.random.fold_in(key, 25), (TOKEN_COUNT // TOK_DEV, HEAD_COUNT), jnp.float32, math.log(0.5), math.log(2.0)))
    block_multiplier = jnp.repeat(block_scale, TOK_DEV, axis=0)
    episodes = jax.random.uniform(jax.random.fold_in(key, 26), (TOKEN_COUNT, 1), jnp.float32) < 3.0 / TOKEN_COUNT
    episode_loss = jnp.log(jax.random.uniform(jax.random.fold_in(key, 27), (TOKEN_COUNT, HEAD_COUNT), jnp.float32, 0.5, 0.8))
    return -(head_decay_rate * random_perturbation * block_multiplier) + jnp.where(episodes, episode_loss, 0.0)


def shard_levels(own_key, dims, split, least, largest):
    factor_of, own = 1.0, jax.random.fold_in(own_key, 6)
    for axis_at, parts in split:
        steps = jnp.exp(jax.random.uniform(jax.random.fold_in(own, axis_at), (parts,), jnp.float32, least / len(split), largest / len(split)))
        factor_of = factor_of * jnp.repeat(steps, dims[axis_at] // parts).reshape([-1 if axis == axis_at else 1 for axis in range(len(dims))])
    return factor_of


def normal_values(rng, dims, spread, bound, pieces=(), held_as=jnp.bfloat16):
    entries = spread * jax.random.normal(rng, dims, jnp.float32)
    if pieces:
        entries = entries * shard_levels(rng, dims, pieces, -0.22, 0.18)
    return jnp.clip(entries, -bound, bound).astype(held_as)


def setup_inputs(seed: int = 0) -> dict:
    seeds = jax.random.split(jax.random.key(seed), 10)
    tokens = draw_tokens(jax.random.fold_in(seeds[9], 71), 0)
    w_latent = normal_values(seeds[1], (D, LAT), D ** -0.5, 0.125, ((1, 4),))
    w_query = normal_values(seeds[2], (D, HEAD_COUNT * DH), D ** -0.5, 0.125, ((1, 4),))
    w_key_up = normal_values(seeds[3], (LAT, HEAD_COUNT * DH), LAT ** -0.5, 0.25, ((1, 4),))
    w_value_up = normal_values(seeds[4], (LAT, HEAD_COUNT * DH), LAT ** -0.5, 0.25, ((1, 4),))
    w_stu_query = normal_values(seeds[5], (D, HEAD_COUNT * DH), D ** -0.5, 0.125, ((1, 4),))
    w_stu_key = normal_values(seeds[6], (D, HEAD_COUNT * DH), D ** -0.5, 0.125, ((1, 4),))
    w_stu_value = normal_values(seeds[7], (D, HEAD_COUNT * DH), D ** -0.5, 0.125, ((1, 4),))
    forget = draw_forget(jax.random.fold_in(seeds[9], 71), 0)
    return {"tokens": tokens, "w_latent": w_latent, "w_query": w_query, "w_key_up": w_key_up, "w_value_up": w_value_up, "w_stu_query": w_stu_query, "w_stu_key": w_stu_key, "w_stu_value": w_stu_value, "forget": forget}


NEG_FILL = -1e+30
EPSILON = 1e-06

def split_heads(matrix):
    return matrix.reshape(matrix.shape[0], HEAD_COUNT, DH)

def unit_rows(matrix):
    return matrix * lax.rsqrt(lax.optimization_barrier(jnp.sum(matrix * matrix, axis=-1, keepdims=True)) + EPSILON)

def reference(tokens, w_latent, w_query, w_key_up, w_value_up, w_stu_query, w_stu_key, w_stu_value, forget):
    highest = lax.Precision.HIGHEST
    latent = jnp.dot(tokens, w_latent, preferred_element_type=jnp.float32).astype(jnp.bfloat16)
    queries = jnp.dot(tokens, w_query, preferred_element_type=jnp.float32).astype(jnp.bfloat16)
    keys = jnp.dot(latent, w_key_up, preferred_element_type=jnp.float32).astype(jnp.bfloat16)
    values = jnp.dot(latent, w_value_up, preferred_element_type=jnp.float32).astype(jnp.bfloat16)
    query_all = split_heads(queries.astype(jnp.float32))
    key_all = split_heads(keys.astype(jnp.float32))
    value_all = split_heads(values.astype(jnp.float32))
    block_size = math.gcd(TOKEN_COUNT, 512)
    block_count = TOKEN_COUNT // block_size
    score_scale = 1.0 / math.sqrt(DH)
    every_pos = jnp.arange(TOKEN_COUNT, dtype=jnp.int32)
    block_ids = jnp.arange(block_count, dtype=jnp.int32)

    def teacher_block(block_index):
        first_row = (block_index * block_size).astype(jnp.int32)
        query_part = lax.dynamic_slice_in_dim(query_all, first_row, block_size, 0)
        scores = jnp.einsum('qhd,khd->hqk', query_part, key_all) * score_scale
        positions = first_row + jnp.arange(block_size, dtype=jnp.int32)
        allowed = every_pos[None, :] <= positions[:, None]
        scores = jnp.where(allowed[None], scores, NEG_FILL)
        row_top = lax.optimization_barrier(jnp.max(scores, axis=2, keepdims=True))
        expos = jnp.where(allowed[None], jnp.exp(scores - row_top), 0.0)
        row_total = lax.optimization_barrier(jnp.sum(expos, axis=2))
        weights = expos.astype(jnp.bfloat16).astype(jnp.float32)
        mixed = jnp.einsum('hqk,khd->qhd', weights, value_all) / row_total.T[:, :, None]
        return mixed.reshape(block_size, HEAD_COUNT * DH).astype(jnp.bfloat16)
    teacher_out = lax.map(teacher_block, block_ids).reshape(TOKEN_COUNT, HEAD_COUNT * DH)
    stu_query = unit_rows(split_heads(jnp.dot(tokens, w_stu_query, preferred_element_type=jnp.float32)))
    stu_key = unit_rows(split_heads(jnp.dot(tokens, w_stu_key, preferred_element_type=jnp.float32)))
    stu_value = split_heads(jnp.dot(tokens, w_stu_value, preferred_element_type=jnp.float32))
    cumul = jnp.cumsum(forget, axis=0)

    def student_block(block_index):
        first_row = (block_index * block_size).astype(jnp.int32)
        query_part = lax.dynamic_slice_in_dim(stu_query, first_row, block_size, 0)
        cumul_part = lax.dynamic_slice_in_dim(cumul, first_row, block_size, 0)
        positions = first_row + jnp.arange(block_size, dtype=jnp.int32)
        allowed = every_pos[None, :] <= positions[:, None]
        scores = jnp.einsum('qhd,khd->hqk', query_part, stu_key, precision=highest)
        log_gap = cumul_part.T[:, :, None] - cumul.T[:, None, :]
        decays = jnp.exp(jnp.where(allowed[None], log_gap, NEG_FILL))
        return jnp.einsum('hqk,khd->qhd', scores * decays, stu_value, precision=highest)
    student_out = lax.map(student_block, block_ids).reshape(TOKEN_COUNT, HEAD_COUNT, DH)
    mismatch = student_out - split_heads(teacher_out.astype(jnp.float32))
    loss_mean = jnp.sum(mismatch * mismatch) / (2.0 * TOKEN_COUNT * HEAD_COUNT * DH)
    grad_out = mismatch / math.sqrt(TOKEN_COUNT)

    def value_block(block_index):
        first_row = (block_index * block_size).astype(jnp.int32)
        key_part = lax.dynamic_slice_in_dim(stu_key, first_row, block_size, 0)
        cumul_part = lax.dynamic_slice_in_dim(cumul, first_row, block_size, 0)
        positions = first_row + jnp.arange(block_size, dtype=jnp.int32)
        allowed = positions[:, None] <= every_pos[None, :]
        scores = jnp.einsum('khd,qhd->hkq', key_part, stu_query, precision=highest)
        log_gap = cumul.T[:, None, :] - cumul_part.T[:, :, None]
        decays = jnp.exp(jnp.where(allowed[None], log_gap, NEG_FILL))
        return jnp.einsum('hkq,qhd->khd', scores * decays, grad_out, precision=highest)
    value_grad = lax.map(value_block, block_ids).reshape(TOKEN_COUNT, HEAD_COUNT * DH).astype(jnp.bfloat16)
    weight_grad = jnp.dot(tokens.T, value_grad, preferred_element_type=jnp.float32)
    return (teacher_out, loss_mean, weight_grad)
```

```python
import functools
import itertools
import math

import jax
import jax.numpy as jnp
from jax import lax
from jax.experimental import pallas as pl
from jax.experimental.pallas import tpu as pltpu
from jax.sharding import PartitionSpec as P

NEG_FILL = -1e30
EPSILON = 1e-06
F32 = jnp.float32
BF16 = jnp.bfloat16


def dot32(a, b, dims=((1,), (0,))):
    return lax.dot_general(a, b, (dims, ((), ())), preferred_element_type=F32)


def swap(value, axis, mask):
    pairs = [(i, i ^ mask) for i in range(lax.axis_size(axis))]
    return lax.ppermute(value, axis, pairs)


def attention_kernel(seq_ref, *refs, groups, subs, scale):
    count = groups * subs
    kv_in, q_in = refs[:count], refs[count : 2 * count]
    out_ref, kv_ref, vt_ref, q_ref, kv_sem, q_sem = refs[2 * count :]
    rows, twice = kv_ref.shape[1:]
    head_size = twice // 2
    piece = q_ref.shape[2]
    group_own = seq_ref[0] // subs
    sub_own = seq_ref[0] % subs

    copies = []
    for m in range(groups):
        for k in range(subs):
            at = m * subs + k
            block = (group_own ^ m) * subs + (sub_own ^ k)
            copies.append(
                (
                    block,
                    pltpu.make_async_copy(kv_in[at], kv_ref.at[block], kv_sem.at[at]),
                    pltpu.make_async_copy(q_in[at], q_ref.at[m, k], q_sem.at[at]),
                )
            )
    for _, first, second in copies:
        first.start()
        second.start()
    for block, first, second in copies:
        first.wait()
        second.wait()
        vt_ref[block] = kv_ref[block, :, head_size:].T

    def per_group(m, _):
        group = group_own ^ m
        q_parts = [q_ref[m, k] for k in range(subs)]

        def step(block, carried, masked):
            key = kv_ref[block, :, :head_size]
            value_t = vt_ref[block]
            result = []
            for k in range(subs):
                best, total, acc = carried[k]
                scores = dot32(key, q_parts[k], ((1,), (1,))) * scale
                if masked:
                    key_at = block * rows + lax.broadcasted_iota(jnp.int32, scores.shape, 0)
                    q_first = (group * subs + (sub_own ^ k)) * rows + k * piece
                    q_at = q_first + lax.broadcasted_iota(jnp.int32, scores.shape, 1)
                    scores = jnp.where(key_at <= q_at, scores, NEG_FILL)
                new_best = jnp.maximum(best, jnp.max(scores, axis=0, keepdims=True))
                expos = jnp.exp2(scores - new_best)
                factor = jnp.exp2(best - new_best)
                total = total * factor + jnp.sum(expos, axis=0, keepdims=True)
                acc = acc * factor + dot32(value_t, expos.astype(BF16))
                result.append((new_best, total, acc))
            return tuple(result)

        start = tuple(
            (
                jnp.full((1, piece), NEG_FILL, F32),
                jnp.zeros((1, piece), F32),
                jnp.zeros((head_size, piece), F32),
            )
            for _ in range(subs)
        )
        first_own = group * subs
        carried = lax.fori_loop(0, first_own, lambda b, c: step(b, c, False), start)
        carried = lax.fori_loop(
            first_own, first_own + subs, lambda b, c: step(b, c, True), carried
        )
        for k in range(subs):
            _, total, acc = carried[k]
            out_ref[k, m] = (acc / total).T.astype(BF16)
        return 0

    lax.fori_loop(0, groups, per_group, 0)


def attention(seq_index, kv_parts, q_parts, groups, subs, scale):
    rows, twice = kv_parts[0].shape
    piece, head_size = q_parts[0].shape
    count = groups * subs
    any_spec = pl.BlockSpec(memory_space=pl.ANY)
    return pl.pallas_call(
        functools.partial(attention_kernel, groups=groups, subs=subs, scale=scale),
        in_specs=[pl.BlockSpec(memory_space=pltpu.SMEM)] + [any_spec] * (2 * count),
        out_specs=pl.BlockSpec(memory_space=pltpu.VMEM),
        out_shape=jax.ShapeDtypeStruct((subs, groups, piece, head_size), BF16),
        scratch_shapes=[
            pltpu.VMEM((count, rows, twice), BF16),
            pltpu.VMEM((count, head_size, rows), BF16),
            pltpu.VMEM((groups, subs, piece, head_size), BF16),
            pltpu.SemaphoreType.DMA((count,)),
            pltpu.SemaphoreType.DMA((count,)),
        ],
        compiler_params=pltpu.CompilerParams(vmem_limit_bytes=40 * 2**20),
        name="teacher_attention",
    )(seq_index.reshape(1), *kv_parts, *q_parts)


def per_device(
    tokens, w_latent, w_query, w_key_up, w_value_up, w_stu_query, w_stu_key, w_stu_value, forget
):
    rows, width = tokens.shape
    heads = forget.shape[1]
    size = w_query.shape[1] // heads
    lat_part = w_latent.shape[1]
    seq_count, tensor_count = lax.axis_size("seq"), lax.axis_size("tensor")
    seq_index, tensor_index = lax.axis_index("seq"), lax.axis_index("tensor")
    subs = seq_count // heads
    group_own = seq_index // subs
    seq_bits = seq_count.bit_length() - 1
    tensor_bits = tensor_count.bit_length() - 1
    piece = rows // subs

    def cols(matrix, at, wide):
        return lax.dynamic_slice_in_dim(matrix, at * wide, wide, 1)

    latent_own = dot32(tokens, w_latent).astype(BF16)
    latent_parts = [latent_own] + [swap(latent_own, "tensor", m) for m in range(1, tensor_count)]

    log_cumul = jnp.cumsum(forget, axis=0)
    block_end = log_cumul[-1:, :]
    own_logs, partner_logs = [block_end], []
    for bit in range(seq_bits):
        partner_logs.append(swap(own_logs[-1], "seq", 1 << bit))
        own_logs.append(own_logs[-1] + partner_logs[-1])
    upper = [((seq_index >> bit) & 1) == 1 for bit in range(seq_bits)]

    def log_of_head(row, h):
        return row[0, h]

    def scan_states(states, from_later):
        total = states
        found = jnp.zeros_like(states)
        reach = jnp.zeros_like(block_end)
        for bit in range(seq_bits):
            got = swap(total.astype(BF16), "seq", 1 << bit).astype(F32)
            own_log, got_log = own_logs[bit], partner_logs[bit]
            takes = jnp.logical_not(upper[bit]) if from_later else upper[bit]
            gain = jnp.where(takes, jnp.exp(reach), 0.0)
            found = found + gain[0][:, None, None] * got
            reach = reach + jnp.where(takes, got_log, 0.0)
            own_factor = jnp.where(takes, 1.0, jnp.exp(got_log))
            got_factor = jnp.where(takes, jnp.exp(own_log), 1.0)
            total = own_factor[0][:, None, None] * total + got_factor[0][:, None, None] * got
        return found

    queries = dot32(tokens, w_query).astype(BF16)
    q_near = []
    for m in range(heads):
        part = cols(queries, group_own ^ m, size)
        q_near.append(swap(part, "seq", m * subs) if m else part)

    def rows_rel(matrix):
        return jnp.concatenate(
            [
                lax.dynamic_slice_in_dim(matrix, (tensor_index ^ m) * lat_part, lat_part, 0)
                for m in range(tensor_count)
            ],
            axis=0,
        )

    key_up, value_up = rows_rel(w_key_up), rows_rel(w_value_up)
    latent = jnp.concatenate(latent_parts, axis=1)
    kv_near = []
    for m in list(range(1, heads)) + [0]:
        head = group_own ^ m
        both = jnp.concatenate([cols(key_up, head, size), cols(value_up, head, size)], axis=1)
        part = dot32(latent, both).astype(BF16)
        kv_near.append(swap(part, "seq", m * subs) if m else part)
    kv_near = kv_near[-1:] + kv_near[:-1]

    kv_parts, q_parts = [], []
    for m in range(heads):
        for k in range(subs):
            q_piece = q_near[m][k * piece : (k + 1) * piece]
            kv_parts.append(swap(kv_near[m], "seq", k) if k else kv_near[m])
            q_parts.append(swap(q_piece, "seq", k) if k else q_piece)

    raw_query = dot32(tokens, w_stu_query)
    raw_key = dot32(tokens, w_stu_key)
    stu_value = dot32(tokens, w_stu_value).astype(BF16)
    log_rows = log_cumul.T
    causal = jnp.arange(rows)[None, :] <= jnp.arange(rows)[:, None]
    start_weight = jnp.exp(log_cumul)
    end_weight = jnp.exp(block_end - log_cumul)

    def head_of(matrix, h):
        return matrix[:, h * size : (h + 1) * size]

    def unit(matrix):
        return matrix * lax.rsqrt(jnp.sum(matrix * matrix, axis=1, keepdims=True) + EPSILON)

    mixing, intra, state_end, query_start, key_end = [], [], [], [], []
    for h in range(heads):
        query, key = unit(head_of(raw_query, h)), unit(head_of(raw_key, h))
        gap = jnp.where(causal, log_cumul[:, h : h + 1] - log_rows[h : h + 1, :], NEG_FILL)
        mix = (dot32(query.astype(BF16), key.astype(BF16), ((1,), (1,))) * jnp.exp(gap)).astype(BF16)
        mixing.append(mix)
        query_start.append((query * start_weight[:, h : h + 1]).astype(BF16))
        key_end.append((key * end_weight[:, h : h + 1]).astype(BF16))
        state_end.append(dot32(key_end[h], head_of(stu_value, h), ((0,), (0,))))
    prefix = scan_states(jnp.stack(state_end), False).astype(BF16)
    student = []
    for h in range(heads):
        student.append(
            dot32(mixing[h], head_of(stu_value, h)) + dot32(query_start[h], prefix[h])
        )

    slab = width // seq_count

    def tokens_rel(bit0):
        members = []
        for digits in itertools.product((0, 1), repeat=seq_bits - 1):
            m = bit0 + sum(d << (a + 1) for a, d in enumerate(digits))
            members.append(cols(tokens, seq_index ^ m, slab))
        return jnp.concatenate(members, axis=1)

    tokens_keep, tokens_send = tokens_rel(0), tokens_rel(1)

    out = attention(
        seq_index, kv_parts, q_parts, heads, subs, math.log2(math.e) / math.sqrt(size)
    )
    out_rows = [out[0]] + [swap(out[k], "seq", k) for k in range(1, subs)]
    out_near = []
    for m in range(heads):
        part = jnp.concatenate([member[m] for member in out_rows], axis=0)
        out_near.append(swap(part, "seq", m * subs) if m else part)
    out_table = jnp.stack(out_near)
    teacher_heads = [
        lax.dynamic_index_in_dim(out_table, group_own ^ h, 0, keepdims=False) for h in range(heads)
    ]
    teacher_out = jnp.concatenate(teacher_heads, axis=1)

    total_rows = seq_count * rows
    mismatch = [student[h] - teacher_heads[h].astype(F32) for h in range(heads)]
    grads = [(member * (1.0 / math.sqrt(total_rows))).astype(BF16) for member in mismatch]
    back_state = jnp.stack(
        [dot32(query_start[h], grads[h], ((0,), (0,))) for h in range(heads)]
    )
    suffix = scan_states(back_state, True).astype(BF16)
    loss_sum = sum(jnp.sum(member * member) for member in mismatch).reshape(1, 1)
    for bit in range(seq_bits):
        loss_sum = loss_sum + swap(loss_sum, "seq", 1 << bit)
    for bit in range(tensor_bits):
        loss_sum = loss_sum + swap(loss_sum, "tensor", 1 << bit)
    loss_mean = loss_sum[0, 0] / (2.0 * total_rows * heads * tensor_count * size)

    value_grad = [
        (dot32(mixing[h], grads[h], ((0,), (0,))) + dot32(key_end[h], suffix[h])).astype(BF16)
        for h in range(heads)
    ]

    half = heads // 2
    bits = list(range(1, seq_bits))
    pieces = []
    for which, order in ((0, bits), (1, bits[::-1])):
        part = jnp.concatenate(value_grad[which * half : (which + 1) * half], axis=1)
        shape = (2,) * (seq_bits - 1) + (slab, part.shape[1])
        got = swap(dot32(tokens_send, part, ((0,), (0,))).astype(BF16), "seq", 1)
        acc = (dot32(tokens_keep, part, ((0,), (0,))) + got.astype(F32)).reshape(shape)
        left = list(bits)
        for bit in order:
            axis = left.index(bit)
            send = lax.index_in_dim(acc, 1, axis, keepdims=False).astype(BF16)
            acc = lax.index_in_dim(acc, 0, axis, keepdims=False)
            acc = acc + swap(send, "seq", 1 << bit).astype(F32)
            left.remove(bit)
        pieces.append(acc)
    weight_grad = jnp.concatenate(pieces, axis=1)
    return (teacher_out, loss_mean, weight_grad)


def solution(mesh):
    return jax.shard_map(
        per_device,
        mesh=mesh,
        in_specs=(
            P("seq", None),
            P(None, "tensor"),
            P(None, "tensor"),
            P(None, "tensor"),
            P(None, "tensor"),
            P(None, "tensor"),
            P(None, "tensor"),
            P(None, "tensor"),
            P("seq", "tensor"),
        ),
        out_specs=(P("seq", "tensor"), P(), P("seq", "tensor")),
        check_vma=False,
    )
```

```python
import functools
import itertools
import math

import jax
import jax.numpy as jnp
from jax import lax
from jax.experimental import pallas as pl
from jax.experimental.pallas import tpu as pltpu
from jax.sharding import PartitionSpec as P

NEG_FILL = -1e30
EPSILON = 1e-06
F32 = jnp.float32
BF16 = jnp.bfloat16


def dot32(a, b, dims=((1,), (0,))):
    return lax.dot_general(a, b, (dims, ((), ())), preferred_element_type=F32)


def swap(value, axis, mask):
    pairs = [(i, i ^ mask) for i in range(lax.axis_size(axis))]
    return lax.ppermute(value, axis, pairs)


def tie(*values):
    return lax.optimization_barrier(values)


def attention_kernel(seq_ref, *refs, groups, subs, scale):
    count = groups * subs
    kv_in, q_in = refs[:count], refs[count : 2 * count]
    out_ref, kv_ref, vt_ref, q_ref, kv_sem, q_sem = refs[2 * count :]
    rows, twice = kv_ref.shape[1:]
    head_size = twice // 2
    piece = q_ref.shape[2]
    group_own = seq_ref[0] // subs
    sub_own = seq_ref[0] % subs

    copies = []
    for m in range(groups):
        for k in range(subs):
            at = m * subs + k
            block = (group_own ^ m) * subs + (sub_own ^ k)
            copies.append(
                (
                    block,
                    pltpu.make_async_copy(kv_in[at], kv_ref.at[block], kv_sem.at[at]),
                    pltpu.make_async_copy(q_in[at], q_ref.at[m, k], q_sem.at[at]),
                )
            )
    for _, first, second in copies:
        first.start()
        second.start()
    for block, first, second in copies:
        first.wait()
        second.wait()
        vt_ref[block] = kv_ref[block, :, head_size:].T

    def per_group(m, _):
        group = group_own ^ m
        q_parts = [q_ref[m, k] for k in range(subs)]

        def step(block, carried, masked):
            key = kv_ref[block, :, :head_size]
            value_t = vt_ref[block]
            result = []
            for k in range(subs):
                best, total, acc = carried[k]
                scores = dot32(key, q_parts[k], ((1,), (1,))) * scale
                if masked:
                    key_at = block * rows + lax.broadcasted_iota(jnp.int32, scores.shape, 0)
                    q_first = (group * subs + (sub_own ^ k)) * rows + k * piece
                    q_at = q_first + lax.broadcasted_iota(jnp.int32, scores.shape, 1)
                    scores = jnp.where(key_at <= q_at, scores, NEG_FILL)
                new_best = jnp.maximum(best, jnp.max(scores, axis=0, keepdims=True))
                expos = jnp.exp2(scores - new_best)
                factor = jnp.exp2(best - new_best)
                total = total * factor + jnp.sum(expos, axis=0, keepdims=True)
                acc = acc * factor + dot32(value_t, expos.astype(BF16))
                result.append((new_best, total, acc))
            return tuple(result)

        start = tuple(
            (
                jnp.full((1, piece), NEG_FILL, F32),
                jnp.zeros((1, piece), F32),
                jnp.zeros((head_size, piece), F32),
            )
            for _ in range(subs)
        )
        first_own = group * subs
        carried = lax.fori_loop(0, first_own, lambda b, c: step(b, c, False), start)
        carried = lax.fori_loop(
            first_own, first_own + subs, lambda b, c: step(b, c, True), carried
        )
        for k in range(subs):
            _, total, acc = carried[k]
            out_ref[k, m] = (acc / total).T.astype(BF16)
        return 0

    lax.fori_loop(0, groups, per_group, 0)


def attention(seq_index, kv_parts, q_parts, groups, subs, scale):
    rows, twice = kv_parts[0].shape
    piece, head_size = q_parts[0].shape
    count = groups * subs
    any_spec = pl.BlockSpec(memory_space=pl.ANY)
    return pl.pallas_call(
        functools.partial(attention_kernel, groups=groups, subs=subs, scale=scale),
        in_specs=[pl.BlockSpec(memory_space=pltpu.SMEM)] + [any_spec] * (2 * count),
        out_specs=pl.BlockSpec(memory_space=pltpu.VMEM),
        out_shape=jax.ShapeDtypeStruct((subs, groups, piece, head_size), BF16),
        scratch_shapes=[
            pltpu.VMEM((count, rows, twice), BF16),
            pltpu.VMEM((count, head_size, rows), BF16),
            pltpu.VMEM((groups, subs, piece, head_size), BF16),
            pltpu.SemaphoreType.DMA((count,)),
            pltpu.SemaphoreType.DMA((count,)),
        ],
        compiler_params=pltpu.CompilerParams(vmem_limit_bytes=40 * 2**20),
        name="teacher_attention",
    )(seq_index.reshape(1), *kv_parts, *q_parts)


def per_device(
    tokens, w_latent, w_query, w_key_up, w_value_up, w_stu_query, w_stu_key, w_stu_value, forget
):
    rows, width = tokens.shape
    heads = forget.shape[1]
    size = w_query.shape[1] // heads
    lat_part = w_latent.shape[1]
    seq_count, tensor_count = lax.axis_size("seq"), lax.axis_size("tensor")
    seq_index, tensor_index = lax.axis_index("seq"), lax.axis_index("tensor")
    subs = seq_count // heads
    group_own = seq_index // subs
    seq_bits = seq_count.bit_length() - 1
    tensor_bits = tensor_count.bit_length() - 1
    piece = rows // subs

    def cols(matrix, at, wide):
        return lax.dynamic_slice_in_dim(matrix, at * wide, wide, 1)

    latent_own = dot32(tokens, w_latent).astype(BF16)
    latent_parts = [latent_own] + [swap(latent_own, "tensor", m) for m in range(1, tensor_count)]

    log_cumul = jnp.cumsum(forget, axis=0)
    block_end = log_cumul[-1:, :]
    own_logs, partner_logs = [block_end], []
    for bit in range(seq_bits):
        partner_logs.append(swap(own_logs[-1], "seq", 1 << bit))
        own_logs.append(own_logs[-1] + partner_logs[-1])
    upper = [((seq_index >> bit) & 1) == 1 for bit in range(seq_bits)]

    def log_of_head(row, h):
        return row[0, h]

    def scan_states(states, from_later, rider=None):
        total = states
        found = jnp.zeros_like(states)
        reach = jnp.zeros_like(block_end)
        for bit in range(seq_bits):
            send = total.astype(BF16)
            if rider is None:
                got = swap(send, "seq", 1 << bit).astype(F32)
            else:
                send, rider = tie(send, rider)
                got, ride = tie(swap(send, "seq", 1 << bit), swap(rider, "seq", 1 << bit))
                got, rider = got.astype(F32), rider + ride
            own_log, got_log = own_logs[bit], partner_logs[bit]
            takes = jnp.logical_not(upper[bit]) if from_later else upper[bit]
            gain = jnp.where(takes, jnp.exp(reach), 0.0)
            found = found + gain[0][:, None, None] * got
            reach = reach + jnp.where(takes, got_log, 0.0)
            own_factor = jnp.where(takes, 1.0, jnp.exp(got_log))
            got_factor = jnp.where(takes, jnp.exp(own_log), 1.0)
            total = own_factor[0][:, None, None] * total + got_factor[0][:, None, None] * got
        return found if rider is None else (found, rider)

    queries = dot32(tokens, w_query).astype(BF16)
    q_near = []
    for m in range(heads):
        part = cols(queries, group_own ^ m, size)
        q_near.append(swap(part, "seq", m * subs) if m else part)

    def rows_rel(matrix):
        return jnp.concatenate(
            [
                lax.dynamic_slice_in_dim(matrix, (tensor_index ^ m) * lat_part, lat_part, 0)
                for m in range(tensor_count)
            ],
            axis=0,
        )

    key_up, value_up = rows_rel(w_key_up), rows_rel(w_value_up)
    latent = jnp.concatenate(latent_parts, axis=1)
    kv_near, kv_sent = [], []
    for m in list(range(1, heads)) + [0]:
        head = group_own ^ m
        both = jnp.concatenate([cols(key_up, head, size), cols(value_up, head, size)], axis=1)
        part = dot32(latent, both).astype(BF16)
        kv_sent.append(part)
        kv_near.append(swap(part, "seq", m * subs) if m else part)
    kv_near = kv_near[-1:] + kv_near[:-1]

    raw_query = dot32(tokens, w_stu_query)
    tokens_later = tie(tokens, *kv_sent)[0]
    raw_key = dot32(tokens_later, w_stu_key)
    stu_value = dot32(tokens_later, w_stu_value).astype(BF16)
    log_rows = log_cumul.T
    causal = jnp.arange(rows)[None, :] <= jnp.arange(rows)[:, None]
    start_weight = jnp.exp(log_cumul)
    end_weight = jnp.exp(block_end - log_cumul)

    def head_of(matrix, h):
        return matrix[:, h * size : (h + 1) * size]

    def unit(matrix):
        return matrix * lax.rsqrt(jnp.sum(matrix * matrix, axis=1, keepdims=True) + EPSILON)

    half = heads // 2
    keys = [unit(head_of(raw_key, h)) for h in range(heads)]
    key_end = [(keys[h] * end_weight[:, h : h + 1]).astype(BF16) for h in range(heads)]
    state_end = [dot32(key_end[h], head_of(stu_value, h), ((0,), (0,))) for h in range(heads)]
    prefix = scan_states(jnp.stack(state_end), False).astype(BF16)
    mixing, query_start = [], []
    for h in range(heads):
        if h == half:
            tied = tie(*kv_near, *q_near, *mixing, raw_query)
            kv_near, q_near = tied[:heads], tied[heads : 2 * heads]
            mixing, raw_query = list(tied[2 * heads : -1]), tied[-1]
        query = unit(head_of(raw_query, h))
        gap = jnp.where(causal, log_cumul[:, h : h + 1] - log_rows[h : h + 1, :], NEG_FILL)
        scores = dot32(query.astype(BF16), keys[h].astype(BF16), ((1,), (1,)))
        mixing.append((scores * jnp.exp(gap)).astype(BF16))
        query_start.append((query * start_weight[:, h : h + 1]).astype(BF16))
    student = []
    for h in range(heads):
        student.append(
            dot32(mixing[h], head_of(stu_value, h)) + dot32(query_start[h], prefix[h])
        )

    kv_parts, q_parts = [], []
    for m in range(heads):
        for k in range(subs):
            q_piece = q_near[m][k * piece : (k + 1) * piece]
            kv_parts.append(swap(kv_near[m], "seq", k) if k else kv_near[m])
            q_parts.append(swap(q_piece, "seq", k) if k else q_piece)

    slab = width // seq_count

    def tokens_rel(bit0):
        members = []
        for digits in itertools.product((0, 1), repeat=seq_bits - 1):
            m = bit0 + sum(d << (a + 1) for a, d in enumerate(digits))
            members.append(cols(tokens, seq_index ^ m, slab))
        return jnp.concatenate(members, axis=1)

    tokens_keep, tokens_send = tokens_rel(0), tokens_rel(1)

    tied = tie(kv_parts[0], tokens_keep, tokens_send, *student)
    kv_parts[0], tokens_keep, tokens_send, student = tied[0], tied[1], tied[2], tied[3:]

    out = attention(
        seq_index, kv_parts, q_parts, heads, subs, math.log2(math.e) / math.sqrt(size)
    )
    out_rows = [out[0]] + [swap(out[k], "seq", k) for k in range(1, subs)]
    out_near = []
    for m in range(heads):
        part = jnp.concatenate([member[m] for member in out_rows], axis=0)
        out_near.append(swap(part, "seq", m * subs) if m else part)
    out_table = jnp.stack(out_near)
    teacher_heads = [
        lax.dynamic_index_in_dim(out_table, group_own ^ h, 0, keepdims=False) for h in range(heads)
    ]
    teacher_out = jnp.concatenate(teacher_heads, axis=1)

    total_rows = seq_count * rows
    mismatch = [student[h] - teacher_heads[h].astype(F32) for h in range(heads)]
    grads = [(member * (1.0 / math.sqrt(total_rows))).astype(BF16) for member in mismatch]
    back_state = jnp.stack(
        [dot32(query_start[h], grads[h], ((0,), (0,))) for h in range(heads)]
    )
    loss_sum = sum(jnp.sum(member * member) for member in mismatch).reshape(1, 1)
    suffix, loss_sum = scan_states(back_state, True, loss_sum)
    suffix = suffix.astype(BF16)

    value_grad = [
        (dot32(mixing[h], grads[h], ((0,), (0,))) + dot32(key_end[h], suffix[h])).astype(BF16)
        for h in range(heads)
    ]

    bits = list(range(1, seq_bits))
    parts = [jnp.concatenate(value_grad[at : at + half], axis=1) for at in range(0, heads, half)]
    sends = [dot32(tokens_send, part, ((0,), (0,))).astype(BF16) for part in parts]
    loss_bits = list(range(tensor_bits))
    firsts = [swap(send, "seq", 1) for send in sends]
    sends[0], loss_sum = tie(sends[0], loss_sum)
    for bit in loss_bits:
        loss_sum = loss_sum + swap(loss_sum, "tensor", 1 << bit)
    keeps = [dot32(tokens_keep, part, ((0,), (0,))) for part in parts]
    keeps = tie(*keeps)
    pieces = []
    for part, keep, got, order in zip(parts, keeps, firsts, (bits, bits[::-1])):
        shape = (2,) * (seq_bits - 1) + (slab, part.shape[1])
        acc = (keep + got.astype(F32)).reshape(shape)
        left = list(bits)
        for bit in order:
            axis = left.index(bit)
            send = lax.index_in_dim(acc, 1, axis, keepdims=False).astype(BF16)
            acc = lax.index_in_dim(acc, 0, axis, keepdims=False)
            acc = acc + swap(send, "seq", 1 << bit).astype(F32)
            left.remove(bit)
        pieces.append(acc)
    loss_mean = loss_sum[0, 0] / (2.0 * total_rows * heads * tensor_count * size)
    weight_grad = jnp.concatenate(pieces, axis=1)
    return (teacher_out, loss_mean, weight_grad)


def solution(mesh):
    return jax.shard_map(
        per_device,
        mesh=mesh,
        in_specs=(
            P("seq", None),
            P(None, "tensor"),
            P(None, "tensor"),
            P(None, "tensor"),
            P(None, "tensor"),
            P(None, "tensor"),
            P(None, "tensor"),
            P(None, "tensor"),
            P("seq", "tensor"),
        ),
        out_specs=(P("seq", "tensor"), P(), P("seq", "tensor")),
        check_vma=False,
    )
```

```python
import functools
import itertools
import math

import jax
import jax.numpy as jnp
from jax import lax
from jax.experimental import pallas as pl
from jax.experimental.pallas import tpu as pltpu
from jax.sharding import PartitionSpec as P

NEG_FILL = -1e30
EPSILON = 1e-06
F32 = jnp.float32
BF16 = jnp.bfloat16


def dot32(a, b, dims=((1,), (0,))):
    return lax.dot_general(a, b, (dims, ((), ())), preferred_element_type=F32)


def swap(value, axis, mask):
    pairs = [(i, i ^ mask) for i in range(lax.axis_size(axis))]
    return lax.ppermute(value, axis, pairs)


def tie(*values):
    return lax.optimization_barrier(values)


def attention_kernel(seq_ref, *refs, groups, subs, scale):
    count = groups * subs
    kv_in, q_in = refs[:count], refs[count : 2 * count]
    out_ref, kv_ref, vt_ref, q_ref, kv_sem, q_sem = refs[2 * count :]
    rows, twice = kv_ref.shape[1:]
    head_size = twice // 2
    piece = q_ref.shape[2]
    group_own = seq_ref[0] // subs
    sub_own = seq_ref[0] % subs

    copies = []
    for m in range(groups):
        for k in range(subs):
            at = m * subs + k
            block = (group_own ^ m) * subs + (sub_own ^ k)
            copies.append(
                (
                    block,
                    pltpu.make_async_copy(kv_in[at], kv_ref.at[block], kv_sem.at[at]),
                    pltpu.make_async_copy(q_in[at], q_ref.at[m, k], q_sem.at[at]),
                )
            )
    for _, first, second in copies:
        first.start()
        second.start()
    for block, first, second in copies:
        first.wait()
        second.wait()
        vt_ref[block] = kv_ref[block, :, head_size:].T

    shape = (rows, piece)
    offset = lax.broadcasted_iota(jnp.int32, shape, 0) - lax.broadcasted_iota(jnp.int32, shape, 1)

    def per_group(m, _):
        group = group_own ^ m
        q_parts = [q_ref[m, k] for k in range(subs)]

        def step(block, carried, masked):
            key = kv_ref[block, :, :head_size]
            value_t = vt_ref[block]
            result = []
            products = [dot32(key, q_parts[k], ((1,), (1,))) for k in range(subs)]
            for k in range(subs):
                best, total, acc = carried[k]
                scores = products[k] * scale
                if masked:
                    q_first = (group * subs + (sub_own ^ k)) * rows + k * piece
                    scores = jnp.where(offset <= q_first - block * rows, scores, NEG_FILL)
                new_best = jnp.maximum(best, jnp.max(scores, axis=0, keepdims=True))
                expos = jnp.exp2(scores - new_best)
                factor = jnp.exp2(best - new_best)
                total = total * factor + jnp.sum(expos, axis=0, keepdims=True)
                acc = acc * factor + dot32(value_t, expos.astype(BF16))
                result.append((new_best, total, acc))
            return tuple(result)

        start = tuple(
            (
                jnp.full((1, piece), NEG_FILL, F32),
                jnp.zeros((1, piece), F32),
                jnp.zeros((head_size, piece), F32),
            )
            for _ in range(subs)
        )
        def steps(at, carried, masked):
            for k in range(subs):
                carried = step(at * subs + k, carried, masked)
            return carried

        carried = lax.fori_loop(0, group, lambda at, c: steps(at, c, False), start)
        carried = steps(group, carried, True)
        for k in range(subs):
            _, total, acc = carried[k]
            out_ref[k, m] = (acc / total).T.astype(BF16)
        return 0

    lax.fori_loop(0, groups, per_group, 0)


def attention(seq_index, kv_parts, q_parts, groups, subs, scale):
    rows, twice = kv_parts[0].shape
    piece, head_size = q_parts[0].shape
    count = groups * subs
    any_spec = pl.BlockSpec(memory_space=pl.ANY)
    return pl.pallas_call(
        functools.partial(attention_kernel, groups=groups, subs=subs, scale=scale),
        in_specs=[pl.BlockSpec(memory_space=pltpu.SMEM)] + [any_spec] * (2 * count),
        out_specs=pl.BlockSpec(memory_space=pltpu.VMEM),
        out_shape=jax.ShapeDtypeStruct((subs, groups, piece, head_size), BF16),
        scratch_shapes=[
            pltpu.VMEM((count, rows, twice), BF16),
            pltpu.VMEM((count, head_size, rows), BF16),
            pltpu.VMEM((groups, subs, piece, head_size), BF16),
            pltpu.SemaphoreType.DMA((count,)),
            pltpu.SemaphoreType.DMA((count,)),
        ],
        compiler_params=pltpu.CompilerParams(vmem_limit_bytes=40 * 2**20),
        name="teacher_attention",
    )(seq_index.reshape(1), *kv_parts, *q_parts)


def per_device(
    tokens, w_latent, w_query, w_key_up, w_value_up, w_stu_query, w_stu_key, w_stu_value, forget
):
    rows, width = tokens.shape
    heads = forget.shape[1]
    size = w_query.shape[1] // heads
    lat_part = w_latent.shape[1]
    seq_count, tensor_count = lax.axis_size("seq"), lax.axis_size("tensor")
    seq_index, tensor_index = lax.axis_index("seq"), lax.axis_index("tensor")
    subs = seq_count // heads
    group_own = seq_index // subs
    seq_bits = seq_count.bit_length() - 1
    tensor_bits = tensor_count.bit_length() - 1
    piece = rows // subs

    def cols(matrix, at, wide):
        return lax.dynamic_slice_in_dim(matrix, at * wide, wide, 1)

    latent_own = dot32(tokens, w_latent).astype(BF16)
    latent_parts = [latent_own] + [swap(latent_own, "tensor", m) for m in range(1, tensor_count)]

    log_cumul = jnp.cumsum(forget, axis=0)
    block_end = log_cumul[-1:, :]
    upper = [((seq_index >> bit) & 1) == 1 for bit in range(seq_bits)]

    def in_parts(value):
        terms = []
        for _ in range(3):
            terms.append(lax.reduce_precision(value, 8, 7))
            value = value - terms[-1]
        lane = lax.broadcasted_iota(jnp.int32, (16, size), 1)
        first = lax.broadcasted_iota(jnp.int32, (16, size), 0) == 0
        packed = jnp.zeros((16, size), F32)
        for at, term in enumerate(terms):
            packed = jnp.where(first & (lane == at), term, packed)
        return packed.astype(BF16)

    def scan_states(states, from_later, rider=None):
        total = states
        found = jnp.zeros_like(states)
        reach = jnp.zeros_like(block_end)
        for bit in range(seq_bits):
            send = total.astype(BF16)
            if rider is None:
                got = swap(send, "seq", 1 << bit).astype(F32)
            else:
                flat = send.reshape(heads * size, size)
                got = swap(jnp.concatenate([flat, in_parts(rider)]), "seq", 1 << bit).astype(F32)
                rider = rider + jnp.sum(got[heads * size :])
                got = got[: heads * size].reshape(send.shape)
            own_log, got_log = own_logs[bit], partner_logs[bit]
            takes = jnp.logical_not(upper[bit]) if from_later else upper[bit]
            gain = jnp.where(takes, jnp.exp(reach), 0.0)
            found = found + gain[0][:, None, None] * got
            reach = reach + jnp.where(takes, got_log, 0.0)
            own_factor = jnp.where(takes, 1.0, jnp.exp(got_log))
            got_factor = jnp.where(takes, jnp.exp(own_log), 1.0)
            total = own_factor[0][:, None, None] * total + got_factor[0][:, None, None] * got
        return found if rider is None else (found, rider)

    queries = dot32(tokens, w_query).astype(BF16)
    q_near = []
    for m in range(heads):
        part = cols(queries, group_own ^ m, size)
        q_near.append(swap(part, "seq", m * subs) if m else part)

    def rows_rel(matrix):
        return jnp.concatenate(
            [
                lax.dynamic_slice_in_dim(matrix, (tensor_index ^ m) * lat_part, lat_part, 0)
                for m in range(tensor_count)
            ],
            axis=0,
        )

    key_up, value_up = rows_rel(w_key_up), rows_rel(w_value_up)
    latent = jnp.concatenate(latent_parts, axis=1)
    kv_near, kv_sent = [], []
    for m in list(range(1, heads)) + [0]:
        head = group_own ^ m
        both = jnp.concatenate([cols(key_up, head, size), cols(value_up, head, size)], axis=1)
        part = dot32(latent, both).astype(BF16)
        kv_sent.append(part)
        kv_near.append(swap(part, "seq", m * subs) if m else part)
    kv_near = kv_near[-1:] + kv_near[:-1]

    raw_query = dot32(tokens, w_stu_query)
    tokens_later, block_end = tie(tokens, block_end, *kv_sent)[:2]
    own_logs, partner_logs = [block_end], []
    for bit in range(seq_bits):
        partner_logs.append(swap(own_logs[-1], "seq", 1 << bit))
        own_logs.append(own_logs[-1] + partner_logs[-1])
    raw_key = dot32(tokens_later, w_stu_key)
    stu_value = dot32(tokens_later, w_stu_value).astype(BF16)
    log_rows = log_cumul.T
    causal = jnp.arange(rows)[None, :] <= jnp.arange(rows)[:, None]
    start_weight = jnp.exp(log_cumul)
    end_weight = jnp.exp(block_end - log_cumul)

    def head_of(matrix, h):
        return matrix[:, h * size : (h + 1) * size]

    def unit(matrix):
        return matrix * lax.rsqrt(jnp.sum(matrix * matrix, axis=1, keepdims=True) + EPSILON)

    half = heads // 2
    keys = [unit(head_of(raw_key, h)) for h in range(heads)]
    key_end = [(keys[h] * end_weight[:, h : h + 1]).astype(BF16) for h in range(heads)]
    state_end = [dot32(key_end[h], head_of(stu_value, h), ((0,), (0,))) for h in range(heads)]
    prefix = scan_states(jnp.stack(state_end), False).astype(BF16)
    mixing, query_start = [], []
    for h in range(heads):
        if h == half:
            tied = tie(*kv_near, *q_near, *mixing, raw_query)
            kv_near, q_near = tied[:heads], tied[heads : 2 * heads]
            mixing, raw_query = list(tied[2 * heads : -1]), tied[-1]
        query = unit(head_of(raw_query, h))
        gap = jnp.where(causal, log_cumul[:, h : h + 1] - log_rows[h : h + 1, :], NEG_FILL)
        scores = dot32(query.astype(BF16), keys[h].astype(BF16), ((1,), (1,)))
        mixing.append((scores * jnp.exp(gap)).astype(BF16))
        query_start.append((query * start_weight[:, h : h + 1]).astype(BF16))
    student = []
    for h in range(heads):
        student.append(
            dot32(mixing[h], head_of(stu_value, h)) + dot32(query_start[h], prefix[h])
        )

    kv_parts, q_parts = [], []
    for m in range(heads):
        for k in range(subs):
            q_piece = q_near[m][k * piece : (k + 1) * piece]
            kv_parts.append(swap(kv_near[m], "seq", k) if k else kv_near[m])
            q_parts.append(swap(q_piece, "seq", k) if k else q_piece)

    slab = width // seq_count

    def tokens_rel(bit0):
        members = []
        for digits in itertools.product((0, 1), repeat=seq_bits - 1):
            m = bit0 + sum(d << (a + 1) for a, d in enumerate(digits))
            members.append(cols(tokens_later, seq_index ^ m, slab))
        return jnp.concatenate(members, axis=1)

    tokens_keep, tokens_send = tokens_rel(0), tokens_rel(1)

    tied = tie(kv_parts[0], tokens_keep, tokens_send, *student)
    kv_parts[0], tokens_keep, tokens_send, student = tied[0], tied[1], tied[2], tied[3:]

    out = attention(
        seq_index, kv_parts, q_parts, heads, subs, math.log2(math.e) / math.sqrt(size)
    )
    out_rows = [out[0]] + [swap(out[k], "seq", k) for k in range(1, subs)]
    out_near = []
    for m in range(heads):
        part = jnp.concatenate([member[m] for member in out_rows], axis=0)
        out_near.append(swap(part, "seq", m * subs) if m else part)
    out_table = jnp.stack(out_near)
    teacher_heads = [
        lax.dynamic_index_in_dim(out_table, group_own ^ h, 0, keepdims=False) for h in range(heads)
    ]
    teacher_out = jnp.concatenate(teacher_heads, axis=1)

    total_rows = seq_count * rows
    mismatch = [student[h] - teacher_heads[h].astype(F32) for h in range(heads)]
    grads = [(member * (1.0 / math.sqrt(total_rows))).astype(BF16) for member in mismatch]
    back_state = jnp.stack(
        [dot32(query_start[h], grads[h], ((0,), (0,))) for h in range(heads)]
    )
    loss_sum = sum(jnp.sum(member * member) for member in mismatch)
    suffix, loss_sum = scan_states(back_state, True, loss_sum)
    suffix = suffix.astype(BF16)

    value_grad = [
        (dot32(mixing[h], grads[h], ((0,), (0,))) + dot32(key_end[h], suffix[h])).astype(BF16)
        for h in range(heads)
    ]

    bits = list(range(1, seq_bits))
    parts = [jnp.concatenate(value_grad[at : at + half], axis=1) for at in range(0, heads, half)]
    sends = [dot32(tokens_send, part, ((0,), (0,))).astype(BF16) for part in parts]
    loss_bits = list(range(tensor_bits))
    firsts = [swap(send, "seq", 1) for send in sends]
    loss_sum = tie(loss_sum.reshape(1, 1), sends[0])[0]
    loss_sum = loss_sum + swap(loss_sum, "tensor", 1 << loss_bits.pop())
    keeps = [dot32(tokens_keep, part, ((0,), (0,))) for part in parts]
    keeps = tie(*keeps)
    pieces = []
    for part, keep, got, order in zip(parts, keeps, firsts, (bits, bits[::-1])):
        shape = (2,) * (seq_bits - 1) + (slab, part.shape[1])
        acc = (keep + got.astype(F32)).reshape(shape)
        left = list(bits)
        for bit in order:
            axis = left.index(bit)
            send = lax.index_in_dim(acc, 1, axis, keepdims=False).astype(BF16)
            acc = lax.index_in_dim(acc, 0, axis, keepdims=False)
            if loss_bits:
                send, loss_sum = tie(send, loss_sum)
                loss_sum = loss_sum + swap(loss_sum, "tensor", 1 << loss_bits.pop())
            acc = acc + swap(send, "seq", 1 << bit).astype(F32)
            left.remove(bit)
        pieces.append(acc)
    for bit in loss_bits:
        loss_sum = loss_sum + swap(loss_sum, "tensor", 1 << bit)
    loss_mean = loss_sum[0, 0] / (2.0 * total_rows * heads * tensor_count * size)
    weight_grad = jnp.concatenate(pieces, axis=1)
    return (teacher_out, loss_mean, weight_grad)


def solution(mesh):
    return jax.shard_map(
        per_device,
        mesh=mesh,
        in_specs=(
            P("seq", None),
            P(None, "tensor"),
            P(None, "tensor"),
            P(None, "tensor"),
            P(None, "tensor"),
            P(None, "tensor"),
            P(None, "tensor"),
            P(None, "tensor"),
            P("seq", "tensor"),
        ),
        out_specs=(P("seq", "tensor"), P(), P("seq", "tensor")),
        check_vma=False,
    )
```
